256 devices in a mesh: peer: 8 (over x, y_hi), space: 32 (over y_lo, z, core).
Axes of the slice: x: 4, y: 4 (y_hi: 2, y_lo: 2; y = y_hi * 2 + y_lo), z: 8, core: 2. Of those that a mesh axis runs over, the one named last changes fastest.
Arguments:
- images: bfloat16 [8, 512, 32, 512], P('peer', 'space'), may hold values from -6 to 6
- task_grad: bfloat16 [8, 512, 32, 512], P('peer', 'space'), may hold values from -6 to 6
- pairing: int32 [8], replicated, may hold values from 0 to 7, as said below
- first_kernel: bfloat16 [8, 3, 3, 512, 512], P('peer'), may hold values from -0.09375 to 0.09375
- first_scale: float32 [8, 512], P('peer'), may hold values from 0.25 to 1.75
- first_shift: float32 [8, 512], P('peer'), may hold values from -3 to 3
- second_kernel: bfloat16 [8, 3, 3, 512, 512], P('peer'), may hold values from -0.09375 to 0.09375
- second_scale: float32 [8, 512], P('peer'), may hold values from 0.25 to 1.75
- second_shift: float32 [8, 512], P('peer'), may hold values from -3 to 3
Outputs:
- input_grad: bfloat16 [8, 512, 32, 512], P('peer', 'space')
The draws below stay inside these ranges and needn't reach their ends.
Inputs may be any that keep to these rules, and one draw needn't show every extreme that they name: `pairing`: every network index appears exactly once.
All inputs are finite; a program needn't handle non-finite values.
Results may differ from the reference program's by a relative error of at most 0.012.
Values may be sent and summed in bfloat16 or wider, within the bound.
A program may use at most 64 MiB of HBM per device.

```python
import jax
import jax.numpy as jnp
from jax import lax

C = 512
W_COLS = 32
H = 512
N_PEER = 8


def swap_entries(order, first_pos, second_pos):
    places = jnp.arange(order.shape[0], dtype=jnp.int32)
    first_val = jnp.sum(jnp.where(places == first_pos, order, 0))
    second_val = jnp.sum(jnp.where(places == second_pos, order, 0))
    order = jnp.where(places == first_pos, second_val, order)
    return jnp.where(places == second_pos, first_val, order)


def draw_pairing(key, part):
    places = jnp.arange(N_PEER, dtype=jnp.int32)
    order = jax.random.permutation(jax.random.fold_in(key, 11), places).astype(jnp.int32)
    anchor = jax.random.randint(jax.random.fold_in(key, 12), (), 0, N_PEER).astype(jnp.int32)
    target = (anchor + N_PEER // 2) % N_PEER
    holder = jnp.sum(jnp.where(order == target, places, 0)).astype(jnp.int32)
    order = swap_entries(order, anchor, holder)
    follower = (anchor + 1) % N_PEER
    holder = jnp.sum(jnp.where(order == anchor, places, 0)).astype(jnp.int32)
    order = swap_entries(order, follower, holder)
    return order.astype(jnp.int32)


def block_levels(rng, shape, cuts, low, largest):
    loudness = 1.0
    for axis_at, parts in cuts:
        steps = jax.random.uniform(jax.random.fold_in(jax.random.fold_in(rng, 6), axis_at), (parts,), jnp.float32, low / len(cuts), largest / len(cuts))
        loudness = loudness * jnp.repeat(jnp.exp(steps), shape[axis_at] // parts).reshape((-1,) + (1,) * (len(shape) - 1 - axis_at))
    return loudness


def scatter_about(own_key, dims, spread, reach, cuts=(), kind=jnp.bfloat16):
    result = spread * jax.random.normal(own_key, dims, jnp.float32)
    if cuts:
        result = result * block_levels(own_key, dims, cuts, -0.22, 0.18)
    return jnp.clip(result, -reach, reach).astype(kind)


def setup_inputs(seed: int = 0) -> dict:
    splits = jax.random.split(jax.random.key(seed), 10)
    return {
        "images": scatter_about(splits[0], (N_PEER, H, W_COLS, C), 1.0, 6.0, ((0, 8), (1, 32))),
        "task_grad": scatter_about(splits[1], (N_PEER, H, W_COLS, C), 1.0, 6.0, ((0, 8), (1, 32))),
        "pairing": draw_pairing(jax.random.fold_in(splits[9], 71), 0),
        "first_kernel": scatter_about(splits[3], (N_PEER, 3, 3, C, C), (9 * C) ** -0.5, 0.09375, ((0, 8),)),
        "first_scale": jnp.clip(1.0 + 0.15 * jax.random.normal(splits[4], (N_PEER, C), jnp.float32), 0.25, 1.75),
        "first_shift": scatter_about(splits[5], (N_PEER, C), 0.5, 3.0, ((0, 8),), jnp.float32),
        "second_kernel": scatter_about(splits[6], (N_PEER, 3, 3, C, C), (9 * C) ** -0.5, 0.09375, ((0, 8),)),
        "second_scale": jnp.clip(1.0 + 0.15 * jax.random.normal(splits[7], (N_PEER, C), jnp.float32), 0.25, 1.75),
        "second_shift": scatter_about(splits[8], (N_PEER, C), 0.5, 3.0, ((0, 8),), jnp.float32),
    }


def apply_dilated_filter(receptive_span, filter_kernel, dilation_rate, reverse_kernel):
    input_rows = receptive_span.shape[0]
    input_width = receptive_span.shape[1]
    padded_input = jnp.pad(receptive_span.astype(jnp.float32), ((dilation_rate, dilation_rate), (dilation_rate, dilation_rate), (0, 0)))
    weights = filter_kernel.astype(jnp.float32)
    total = jnp.zeros((input_rows, input_width, filter_kernel.shape[2]), jnp.float32)
    for kernel_tap_row in range(3):
        for kernel_tap_column in range(3):
            input_window = padded_input[kernel_tap_row * dilation_rate:kernel_tap_row * dilation_rate + input_rows, kernel_tap_column * dilation_rate:kernel_tap_column * dilation_rate + input_width]
            if reverse_kernel:
                total = total + jnp.einsum("rwo,io->rwi", input_window, weights[2 - kernel_tap_row, 2 - kernel_tap_column], precision=lax.Precision.HIGHEST)
            else:
                total = total + jnp.einsum("rwi,io->rwo", input_window, weights[kernel_tap_row, kernel_tap_column], precision=lax.Precision.HIGHEST)
    return total


def silu_slope(value):
    sig = jax.nn.sigmoid(value)
    return sig * (1.0 + value * (1.0 - sig))


def forward_one(image, first_kernel, first_scale, first_shift, second_kernel, second_scale, second_shift):
    pre_first = first_scale * apply_dilated_filter(image, first_kernel, 2, False) + first_shift
    hidden = jax.nn.silu(pre_first).astype(jnp.bfloat16)
    pre_second = second_scale * apply_dilated_filter(hidden, second_kernel, 4, False) + second_shift
    feat = jax.nn.silu(pre_second).astype(jnp.bfloat16)
    return feat


def backward_one(image, task_one, partner_feat, first_kernel, first_scale, first_shift, second_kernel, second_scale, second_shift):
    pre_first = first_scale * apply_dilated_filter(image, first_kernel, 2, False) + first_shift
    hidden = jax.nn.silu(pre_first).astype(jnp.bfloat16)
    pre_second = second_scale * apply_dilated_filter(hidden, second_kernel, 4, False) + second_shift
    feat = jax.nn.silu(pre_second).astype(jnp.bfloat16)
    cot = task_one.astype(jnp.float32) + feat.astype(jnp.float32) - partner_feat.astype(jnp.float32)
    grad_second = (cot * silu_slope(pre_second) * second_scale).astype(jnp.bfloat16)
    grad_hidden = apply_dilated_filter(grad_second, second_kernel, 4, True)
    grad_first = (grad_hidden * silu_slope(pre_first) * first_scale).astype(jnp.bfloat16)
    return apply_dilated_filter(grad_first, first_kernel, 2, True).astype(jnp.bfloat16)


def reference(images, task_grad, pairing, first_kernel, first_scale, first_shift, second_kernel, second_scale, second_shift):
    feats = lax.map(lambda args: forward_one(*args), (images, first_kernel, first_scale, first_shift, second_kernel, second_scale, second_shift))
    partners = jnp.take(feats, pairing.astype(jnp.int32), axis=0)
    return lax.map(lambda args: backward_one(*args), (images, task_grad, partners, first_kernel, first_scale, first_shift, second_kernel, second_scale, second_shift))
```

```python
import jax
import jax.numpy as jnp
from jax import lax
from jax.experimental import pallas as pl
from jax.experimental.pallas import tpu as pltpu
from jax.sharding import PartitionSpec as P

MESH = pl.DeviceIdType.MESH
BF16 = jnp.bfloat16
F32 = jnp.float32

ROWS = 16
COLS = 32
CH = 512
PEERS = 8
SPACE = 32
TAPS = 3
POS = ROWS * COLS


def sigmoid(value):
    return 0.5 + 0.5 * jnp.tanh(0.5 * value)


def span(first, count):
    return pl.ds(first * COLS, count * COLS)


def mul(left, right):
    return jnp.dot(left, right, preferred_element_type=F32)


def mul_t(left, right):
    return lax.dot_general(left, right, (((1,), (1,)), ((), ())), preferred_element_type=F32)


def put_shifted(buf, at, value, step):
    count = value.shape[0]
    col = lax.broadcasted_iota(jnp.int32, value.shape, 0) & (COLS - 1)
    ahead = jnp.where(col >= step, pltpu.roll(value, step, 0), 0.0)
    behind = jnp.where(col < COLS - step, pltpu.roll(value, count - step, 0), 0.0)
    buf[0, at, :] = ahead.astype(BF16)
    buf[2, at, :] = behind.astype(BF16)


def kernel(
    pairing,
    images,
    task_grad,
    first_kernel,
    first_scale,
    first_shift,
    second_kernel,
    second_scale,
    second_shift,
    out,
    w1,
    w2,
    img,
    hid,
    grad2,
    grad1,
    img_halo,
    hid_halo,
    grad2_halo,
    grad1_halo,
    pre1,
    pre2,
    acc,
    task,
    feat_in,
    feat_ed,
    spread_in,
    spread_ed,
    picked_in,
    picked_ed,
    partner_in,
    partner_ed,
    load_sem,
    w1_sem,
    w2_sem,
    halo_send,
    halo_recv,
    swap_send,
    swap_recv,
):
    peer = lax.axis_index("peer")
    place = lax.axis_index("space")
    half = SPACE // 2
    across = lax.rem(place + half, SPACE)
    after = lax.rem(place + 1, SPACE)
    before = lax.rem(place + SPACE - 1, SPACE)

    image_load = pltpu.make_async_copy(images.at[0], img.at[1, span(2, ROWS)], load_sem.at[0])
    image_load.start()
    w1_loads = [
        pltpu.make_async_copy(first_kernel.at[0, a], w1.at[a], w1_sem.at[a]) for a in range(TAPS)
    ]
    w2_loads = [
        pltpu.make_async_copy(second_kernel.at[0, a], w2.at[a], w2_sem.at[a]) for a in range(TAPS)
    ]
    task_load = pltpu.make_async_copy(task_grad.at[0], task, load_sem.at[1])
    for a in (1, 0, 2):
        w1_loads[a].start()

    barrier = pltpu.get_barrier_semaphore()
    for neighbour in (before, after):
        pl.semaphore_signal(barrier, inc=1, device_id=(peer, neighbour), device_id_type=MESH)
    for other in range(PEERS):
        pl.semaphore_signal(barrier, inc=1, device_id=(other, across), device_id_type=MESH)
    pl.semaphore_wait(barrier, 2 + PEERS)

    def halo_copies(stage, head, tail, landing):
        down = pltpu.make_async_remote_copy(
            src_ref=tail,
            dst_ref=landing.at[0],
            send_sem=halo_send.at[stage, 0],
            recv_sem=halo_recv.at[stage, 0],
            device_id=(peer, after),
            device_id_type=MESH,
        )
        up = pltpu.make_async_remote_copy(
            src_ref=head,
            dst_ref=landing.at[1],
            send_sem=halo_send.at[stage, 1],
            recv_sem=halo_recv.at[stage, 1],
            device_id=(peer, before),
            device_id_type=MESH,
        )
        return down, up

    def take_halo(buf, landing, step):
        for side, keep in ((0, place > 0), (1, place < SPACE - 1)):
            at = span(0 if side == 0 else ROWS + step, step)
            value = jnp.where(keep, landing[side].astype(F32), 0.0)
            buf[1, at, :] = value.astype(BF16)
            put_shifted(buf, at, value, step)

    def swap_copies(chunk, phase, source, landing):
        return [
            pltpu.make_async_remote_copy(
                src_ref=source.at[i],
                dst_ref=landing.at[peer],
                send_sem=swap_send.at[chunk, phase, i],
                recv_sem=swap_recv.at[chunk, phase, peer],
                device_id=(i, across),
                device_id_type=MESH,
            )
            for i in range(PEERS)
        ]

    def wait_swap(chunk, phase, source, landing):
        for i in range(PEERS):
            pltpu.make_async_remote_copy(
                src_ref=source.at[i],
                dst_ref=landing.at[i],
                send_sem=swap_send.at[chunk, phase, i],
                recv_sem=swap_recv.at[chunk, phase, i],
                device_id=(i, across),
                device_id_type=MESH,
            ).wait_recv()

    image_halo = halo_copies(0, img.at[1, span(2, 2)], img.at[1, span(ROWS, 2)], img_halo)
    image_load.wait()
    for copy in image_halo:
        copy.start()

    @pl.loop(0, ROWS // 2)
    def _(i):
        at = pl.ds(pl.multiple_of((i * 2 + 2) * COLS, 2 * COLS), 2 * COLS)
        put_shifted(img, at, img[1, at, :].astype(F32), 2)

    w1_loads[1].wait()
    acc[...] = sum(mul(img[b, span(2, ROWS)], w1[1, b]) for b in range(TAPS))
    for load in w2_loads:
        load.start()
    task_load.start()
    w1_loads[0].wait()
    w1_loads[2].wait()
    for copy in image_halo:
        copy.wait_recv()
    take_halo(img, img_halo, 2)
    acc[...] += sum(
        mul(img[b, span(2 * a, ROWS)], w1[a, b]) for a in (0, 2) for b in range(TAPS)
    )

    scale1 = first_scale[...]
    shift1 = first_shift[...]

    @pl.loop(0, ROWS // 2)
    def _(i):
        source = pl.ds(pl.multiple_of(i * 2 * COLS, 2 * COLS), 2 * COLS)
        at = pl.ds(pl.multiple_of((i * 2 + 4) * COLS, 2 * COLS), 2 * COLS)
        value = scale1 * acc[source, :] + shift1
        pre1[source, :] = value
        value = value * sigmoid(value)
        hid[1, at, :] = value.astype(BF16)
        put_shifted(hid, at, value, 4)

    hidden_halo = halo_copies(1, hid.at[1, span(4, 4)], hid.at[1, span(ROWS, 4)], hid_halo)
    for copy in hidden_halo:
        copy.start()

    for load in w2_loads:
        load.wait()
    scale2 = second_scale[...]
    shift2 = second_shift[...]

    acc[span(4, 8)] = sum(
        mul(hid[b, span(4 + 4 * a, 8)], w2[a, b]) for a in range(TAPS) for b in range(TAPS)
    )

    def features(row, piece_buf, piece):
        at = span(row, 1)
        value = scale2 * acc[at, :] + shift2
        pre2[at, :] = value
        piece_buf[piece] = (value * sigmoid(value)).astype(BF16)

    for i in range(PEERS):
        features(4 + i, feat_in, i)
    first_in = swap_copies(0, 0, feat_in, spread_in)
    for copy in first_in:
        copy.start()

    acc[span(0, 4)] = sum(
        mul(hid[b, span(4 * a, 4)], w2[a, b])
        for a, at in ((1, 4), (2, 8))
        for b in range(TAPS)
    )
    acc[span(12, 4)] = sum(
        mul(hid[b, span(12 + 4 * a, 4)], w2[a, b])
        for a in (0, 1)
        for b in range(TAPS)
    )
    for copy in hidden_halo:
        copy.wait_recv()
    take_halo(hid, hid_halo, 4)
    acc[span(0, 4)] += sum(mul(hid[b, span(0, 4)], w2[0, b]) for b in range(TAPS))
    acc[span(12, 4)] += sum(mul(hid[b, span(20, 4)], w2[2, b]) for b in range(TAPS))
    for i in range(PEERS):
        features(i if i < 4 else 8 + i, feat_ed, i)
    first_ed = swap_copies(1, 0, feat_ed, spread_ed)
    for copy in first_ed:
        copy.start()

    def slope(value):
        s = sigmoid(value)
        return s * (1.0 + value * (1.0 - s))

    @pl.loop(0, ROWS)
    def _(i):
        at = pl.ds(pl.multiple_of(i * COLS, COLS), COLS)
        pre1[at, :] = slope(pre1[at, :]) * scale1
        pre2[at, :] = slope(pre2[at, :]) * scale2

    task_load.wait()

    wait_swap(0, 0, feat_in, spread_in)
    for i in range(PEERS):
        picked_in[i] = spread_in[pairing[i]]
    second_in = swap_copies(0, 1, picked_in, partner_in)
    for copy in second_in:
        copy.start()
    wait_swap(1, 0, feat_ed, spread_ed)
    for i in range(PEERS):
        picked_ed[i] = spread_ed[pairing[i]]
    second_ed = swap_copies(1, 1, picked_ed, partner_ed)
    for copy in second_ed:
        copy.start()

    def cotangent(row, feat, partner, piece):
        at = span(row, 1)
        cot = task[row].astype(F32) + feat[piece].astype(F32) - partner[piece].astype(F32)
        value = cot * pre2[at, :]
        to = span(row + 4, 1)
        grad2[1, to, :] = value.astype(BF16)
        put_shifted(grad2, to, value, 4)

    def back2(first, count, a):
        return sum(
            mul_t(grad2[b, span(first + 4, count)], w2[2 - a, 2 - b]) for b in range(TAPS)
        )

    wait_swap(0, 1, picked_in, partner_in)
    for i in range(PEERS):
        cotangent(4 + i, feat_in, partner_in, i)
    acc[span(4, 8)] = back2(4, 8, 1)
    acc[span(0, 4)] = back2(4, 4, 2)
    acc[span(4, 4)] += back2(8, 4, 2)
    acc[span(12, 4)] = back2(8, 4, 0)
    acc[span(8, 4)] += back2(4, 4, 0)

    wait_swap(1, 1, picked_ed, partner_ed)
    for i in range(PEERS):
        cotangent(i if i < 4 else 8 + i, feat_ed, partner_ed, i)
    cot_halo = halo_copies(2, grad2.at[1, span(4, 4)], grad2.at[1, span(ROWS, 4)], grad2_halo)
    for copy in cot_halo:
        copy.start()
    acc[span(0, 4)] += back2(0, 4, 1)
    acc[span(12, 4)] += back2(12, 4, 1)
    acc[span(4, 4)] += back2(0, 4, 0)
    acc[span(8, 4)] += back2(12, 4, 2)
    for copy in cot_halo:
        copy.wait_recv()
    take_halo(grad2, grad2_halo, 4)
    acc[span(0, 4)] += back2(-4, 4, 0)
    acc[span(12, 4)] += back2(16, 4, 2)

    @pl.loop(0, ROWS // 2)
    def _(i):
        source = pl.ds(pl.multiple_of(i * 2 * COLS, 2 * COLS), 2 * COLS)
        at = pl.ds(pl.multiple_of((i * 2 + 2) * COLS, 2 * COLS), 2 * COLS)
        value = acc[source, :] * pre1[source, :]
        grad1[1, at, :] = value.astype(BF16)
        put_shifted(grad1, at, value, 2)

    hid_grad_halo = halo_copies(3, grad1.at[1, span(2, 2)], grad1.at[1, span(ROWS, 2)], grad1_halo)
    for copy in hid_grad_halo:
        copy.start()
    acc[...] = sum(mul_t(grad1[b, span(2, ROWS)], w1[1, 2 - b]) for b in range(TAPS))
    for copy in hid_grad_halo:
        copy.wait_recv()
    take_halo(grad1, grad1_halo, 2)
    out[0] = (
        acc[...]
        + sum(
            mul_t(grad1[b, span(2 * a, ROWS)], w1[2 - a, 2 - b])
            for a in (0, 2)
            for b in range(TAPS)
        )
    ).reshape(ROWS, COLS, CH).astype(BF16)

    for copies in (
        image_halo,
        hidden_halo,
        cot_halo,
        hid_grad_halo,
        first_in,
        first_ed,
        second_in,
        second_ed,
    ):
        for copy in copies:
            copy.wait_send()


def per_device(*args):
    any_spec = pl.BlockSpec(memory_space=pl.ANY)
    vmem = pl.BlockSpec(memory_space=pltpu.VMEM)
    dma = pltpu.SemaphoreType.DMA
    pieces = pltpu.VMEM((PEERS, COLS, CH), BF16)
    return pl.pallas_call(
        kernel,
        out_shape=jax.ShapeDtypeStruct((1, ROWS, COLS, CH), BF16),
        in_specs=[
            pl.BlockSpec(memory_space=pltpu.SMEM),
            any_spec,
            any_spec,
            any_spec,
            vmem,
            vmem,
            any_spec,
            vmem,
            vmem,
        ],
        out_specs=vmem,
        scratch_shapes=[
            pltpu.VMEM((TAPS, TAPS, CH, CH), BF16),
            pltpu.VMEM((TAPS, TAPS, CH, CH), BF16),
            pltpu.VMEM((TAPS, (ROWS + 4) * COLS, CH), BF16),
            pltpu.VMEM((TAPS, (ROWS + 8) * COLS, CH), BF16),
            pltpu.VMEM((TAPS, (ROWS + 8) * COLS, CH), BF16),
            pltpu.VMEM((TAPS, (ROWS + 4) * COLS, CH), BF16),
            pltpu.VMEM((2, 2 * COLS, CH), BF16),
            pltpu.VMEM((2, 4 * COLS, CH), BF16),
            pltpu.VMEM((2, 4 * COLS, CH), BF16),
            pltpu.VMEM((2, 2 * COLS, CH), BF16),
            pltpu.VMEM((POS, CH), F32),
            pltpu.VMEM((POS, CH), F32),
            pltpu.VMEM((POS, CH), F32),
            pltpu.VMEM((ROWS, COLS, CH), BF16),
            pieces,
            pieces,
            pieces,
            pieces,
            pieces,
            pieces,
            pieces,
            pieces,
            dma((2,)),
            dma((TAPS,)),
            dma((TAPS,)),
            dma((4, 2)),
            dma((4, 2)),
            dma((2, 2, PEERS)),
            dma((2, 2, PEERS)),
        ],
        compiler_params=pltpu.CompilerParams(
            collective_id=0, has_side_effects=True, vmem_limit_bytes=56 << 20
        ),
        name="distill",
    )(args[2], args[0].reshape(1, POS, CH), args[1], *args[3:])


def solution(mesh):
    placed = (
        P("peer", "space", None, None),
        P("peer", "space", None, None),
        P(),
        P("peer", None, None, None, None),
        P("peer", None),
        P("peer", None),
        P("peer", None, None, None, None),
        P("peer", None),
        P("peer", None),
    )
    return jax.shard_map(
        per_device,
        mesh=mesh,
        in_specs=placed,
        out_specs=P("peer", "space", None, None),
        check_vma=False,
    )
```

```python
import jax
import jax.numpy as jnp
from jax import lax
from jax.experimental import pallas as pl
from jax.experimental.pallas import tpu as pltpu
from jax.sharding import PartitionSpec as P

MESH = pl.DeviceIdType.MESH
BF16 = jnp.bfloat16
F32 = jnp.float32

ROWS = 16
COLS = 32
CH = 512
PEERS = 8
SPACE = 32
TAPS = 3
POS = ROWS * COLS
HALF = CH // 2
EDGE = (0, 1, 2, 3, 12, 13, 14, 15)
INNER = tuple(range(4, 12))
LANES = (pl.ds(0, HALF), pl.ds(HALF, HALF))
CHUNKS = ((INNER, 0), (INNER, 1), (EDGE, 0), (EDGE, 1))


def sigmoid(value):
    return 0.5 + 0.5 * jnp.tanh(0.5 * value)


def span(first, count):
    return pl.ds(first * COLS, count * COLS)


def mul(left, right):
    return jnp.dot(left, right, preferred_element_type=F32)


def mul_t(left, right):
    return lax.dot_general(left, right, (((1,), (1,)), ((), ())), preferred_element_type=F32)


def put_shifted(buf, at, value, step, lanes=slice(None)):
    count = value.shape[0]
    col = lax.broadcasted_iota(jnp.int32, value.shape, 0) & (COLS - 1)
    ahead = jnp.where(col >= step, pltpu.roll(value, step, 0), 0.0)
    behind = jnp.where(col < COLS - step, pltpu.roll(value, count - step, 0), 0.0)
    buf[0, at, lanes] = ahead.astype(BF16)
    buf[2, at, lanes] = behind.astype(BF16)


def kernel(
    pairing_in,
    images,
    task_grad,
    first_kernel,
    first_scale,
    first_shift,
    second_kernel,
    second_scale,
    second_shift,
    out,
    pairing,
    norms,
    w1,
    w2,
    img,
    hid,
    grad2,
    grad1,
    img_halo,
    hid_halo,
    grad2_halo_a,
    grad2_halo_b,
    grad1_halo,
    pre1,
    pre2,
    acc,
    task,
    *rest,
):
    feat, spread, picked, partner = (rest[4 * i : 4 * i + 4] for i in range(4))
    load_sem, w1_sem, w2_sem, halo_send, halo_recv, swap_send, swap_recv = rest[16:]
    peer = lax.axis_index("peer")
    place = lax.axis_index("space")
    across = lax.rem(place + SPACE // 2, SPACE)
    after = lax.rem(place + 1, SPACE)
    before = lax.rem(place + SPACE - 1, SPACE)
    has_after = place < SPACE - 1
    has_before = place > 0

    image_load = pltpu.make_async_copy(images.at[0], img.at[1, span(2, ROWS)], load_sem.at[0])
    image_load.start()
    w1_loads = [
        pltpu.make_async_copy(first_kernel.at[0, a], w1.at[a], w1_sem.at[a]) for a in range(TAPS)
    ]
    w2_loads = [
        pltpu.make_async_copy(second_kernel.at[0, a], w2.at[a], w2_sem.at[a]) for a in range(TAPS)
    ]
    task_load = pltpu.make_async_copy(task_grad.at[0], task, load_sem.at[1])
    for a in (1, 0, 2):
        w1_loads[a].start()
    small_loads = [
        pltpu.make_async_copy(array, norms.at[i], load_sem.at[2 + i])
        for i, array in enumerate((first_scale, first_shift, second_scale, second_shift))
    ]
    small_loads.append(pltpu.make_async_copy(pairing_in, pairing, load_sem.at[6]))
    for load in small_loads:
        load.start()

    barrier = pltpu.get_barrier_semaphore()
    for neighbour in (before, after):
        pl.semaphore_signal(barrier, inc=1, device_id=(peer, neighbour), device_id_type=MESH)
    for other in range(PEERS):
        pl.semaphore_signal(barrier, inc=1, device_id=(other, across), device_id_type=MESH)

    landings = (img_halo, hid_halo, grad2_halo_a, grad2_halo_b, grad1_halo)
    for side, missing in ((0, place == 0), (1, place == SPACE - 1)):

        @pl.when(missing)
        def _(side=side):
            for landing in landings:
                landing[side] = jnp.zeros(landing.shape[1:], BF16)

    pl.semaphore_wait(barrier, 2 + PEERS)

    def halo_copies(stage, head, tail):
        down = pltpu.make_async_remote_copy(
            src_ref=tail,
            dst_ref=landings[stage].at[0],
            send_sem=halo_send.at[stage, 0],
            recv_sem=halo_recv.at[stage, 0],
            device_id=(peer, after),
            device_id_type=MESH,
        )
        up = pltpu.make_async_remote_copy(
            src_ref=head,
            dst_ref=landings[stage].at[1],
            send_sem=halo_send.at[stage, 1],
            recv_sem=halo_recv.at[stage, 1],
            device_id=(peer, before),
            device_id_type=MESH,
        )

        @pl.when(has_after)
        def _():
            down.start()

        @pl.when(has_before)
        def _():
            up.start()

        return down, up

    def wait_halo(copies):
        down, up = copies

        @pl.when(has_before)
        def _():
            down.wait_recv()

        @pl.when(has_after)
        def _():
            up.wait_recv()

    def take_halo(buf, stage, step, lanes=slice(None)):
        for side in (0, 1):
            at = span(0 if side == 0 else ROWS + step, step)
            value = landings[stage][side]
            buf[1, at, lanes] = value
            put_shifted(buf, at, value.astype(F32), step, lanes)

    def swap_copy(chunk, phase, source, landing, i, slot):
        return pltpu.make_async_remote_copy(
            src_ref=source[chunk].at[i],
            dst_ref=landing[chunk].at[slot],
            send_sem=swap_send.at[chunk, phase, i],
            recv_sem=swap_recv.at[chunk, phase, slot],
            device_id=(i, across),
            device_id_type=MESH,
        )

    def send_pieces(chunk, phase):
        source, landing = ((feat, spread), (picked, partner))[phase]
        for i in range(PEERS):
            swap_copy(chunk, phase, source, landing, i, peer).start()

    def wait_pieces(chunk, phase):
        source, landing = ((feat, spread), (picked, partner))[phase]
        for i in range(PEERS):
            swap_copy(chunk, phase, source, landing, i, i).wait_recv()

    image_halo = halo_copies(0, images.at[0, span(0, 2)], images.at[0, span(ROWS - 2, 2)])

    image_load.wait()

    @pl.loop(0, ROWS // 2)
    def _(i):
        at = pl.ds(pl.multiple_of((i * 2 + 2) * COLS, 2 * COLS), 2 * COLS)
        put_shifted(img, at, img[1, at, :].astype(F32), 2)

    w1_loads[1].wait()
    acc[...] = sum(mul(img[b, span(2, ROWS)], w1[1, b]) for b in range(TAPS))
    for load in w2_loads:
        load.start()
    task_load.start()
    w1_loads[0].wait()
    acc[span(2, ROWS - 2)] += sum(mul(img[b, span(2, ROWS - 2)], w1[0, b]) for b in range(TAPS))
    w1_loads[2].wait()
    acc[span(0, ROWS - 2)] += sum(mul(img[b, span(4, ROWS - 2)], w1[2, b]) for b in range(TAPS))

    for load in small_loads:
        load.wait()
    scale1, shift1, scale2, shift2 = (norms[i] for i in range(4))

    def hidden_rows(first, count):
        @pl.loop(0, count // 2)
        def _(i):
            source = pl.ds(pl.multiple_of((first + i * 2) * COLS, 2 * COLS), 2 * COLS)
            at = pl.ds(pl.multiple_of((first + i * 2 + 4) * COLS, 2 * COLS), 2 * COLS)
            value = scale1 * acc[source, :] + shift1
            pre1[source, :] = value
            value = value * sigmoid(value)
            hid[1, at, :] = value.astype(BF16)
            put_shifted(hid, at, value, 4)

    hidden_rows(4, 8)
    wait_halo(image_halo)
    take_halo(img, 0, 2)
    acc[span(0, 2)] += sum(mul(img[b, span(0, 2)], w1[0, b]) for b in range(TAPS))
    acc[span(ROWS - 2, 2)] += sum(mul(img[b, span(ROWS + 2, 2)], w1[2, b]) for b in range(TAPS))
    hidden_rows(0, 4)
    hidden_rows(12, 4)
    hidden_halo = halo_copies(1, hid.at[1, span(4, 4)], hid.at[1, span(ROWS, 4)])

    for load in w2_loads:
        load.wait()

    def features(chunk):
        rows, half = CHUNKS[chunk]
        lanes = LANES[half]
        scale = scale2[:, half * HALF : (half + 1) * HALF]
        shift = shift2[:, half * HALF : (half + 1) * HALF]
        for i, row in enumerate(rows):
            at = span(row, 1)
            value = scale * acc[at, lanes] + shift
            pre2[at, lanes] = value
            feat[chunk][i] = (value * sigmoid(value)).astype(BF16)
        send_pieces(chunk, 0)

    for half in (0, 1):
        acc[span(4, 8), LANES[half]] = sum(
            mul(hid[b, span(4 + 4 * a, 8)], w2[a, b, :, LANES[half]])
            for a in range(TAPS)
            for b in range(TAPS)
        )
        features(half)

    middle = sum(
        mul(jnp.concatenate([hid[b, span(4, 4)], hid[b, span(16, 4)]], 0), w2[1, b])
        for b in range(TAPS)
    )
    acc[span(0, 4)] = middle[: POS // 4]
    acc[span(12, 4)] = middle[POS // 4 :]
    acc[span(0, 4)] += sum(mul(hid[b, span(8, 4)], w2[2, b]) for b in range(TAPS))
    acc[span(12, 4)] += sum(mul(hid[b, span(12, 4)], w2[0, b]) for b in range(TAPS))
    wait_halo(hidden_halo)
    take_halo(hid, 1, 4)
    for half in (0, 1):
        for row, at, a in ((0, 0, 0), (12, 20, 2)):
            acc[span(row, 4), LANES[half]] += sum(
                mul(hid[b, span(at, 4)], w2[a, b, :, LANES[half]]) for b in range(TAPS)
            )
        features(2 + half)

    def slope(value):
        s = sigmoid(value)
        return s * (1.0 + value * (1.0 - s))

    @pl.loop(0, ROWS)
    def _(i):
        at = pl.ds(pl.multiple_of(i * COLS, COLS), COLS)
        pre2[at, :] = slope(pre2[at, :]) * scale2
        pre1[at, :] = slope(pre1[at, :]) * scale1

    task_load.wait()

    def pass_on(chunk):
        wait_pieces(chunk, 0)
        for i in range(PEERS):
            picked[chunk][i] = spread[chunk][pairing[i]]
        send_pieces(chunk, 1)

    for chunk in (2, 3, 0, 1):
        pass_on(chunk)

    def cotangent(chunk):
        rows, half = CHUNKS[chunk]
        lanes = LANES[half]
        wait_pieces(chunk, 1)
        for i, row in enumerate(rows):
            cot = task[row, :, lanes].astype(F32) + feat[chunk][i].astype(F32)
            value = (cot - partner[chunk][i].astype(F32)) * pre2[span(row, 1), lanes]
            to = span(row + 4, 1)
            grad2[1, to, lanes] = value.astype(BF16)
            put_shifted(grad2, to, value, 4, lanes)

    def back2(first, count, a, half):
        lanes = LANES[half]
        return sum(
            mul_t(grad2[b, span(first + 4, count), lanes], w2[2 - a, 2 - b, :, lanes])
            for b in range(TAPS)
        )

    cot_halo = []
    for half in (0, 1):
        lanes = LANES[half]
        cotangent(2 + half)
        cot_halo.append(
            halo_copies(
                2 + half, grad2.at[1, span(4, 4), lanes], grad2.at[1, span(ROWS, 4), lanes]
            )
        )
        middle = sum(
            mul_t(
                jnp.concatenate([grad2[b, span(4, 4), lanes], grad2[b, span(16, 4), lanes]], 0),
                w2[1, 2 - b, :, lanes],
            )
            for b in range(TAPS)
        )
        if half == 0:
            acc[span(0, 4)] = middle[: POS // 4]
            acc[span(12, 4)] = middle[POS // 4 :]
            acc[span(4, 4)] = back2(0, 4, 0, half)
            acc[span(8, 4)] = back2(12, 4, 2, half)
        else:
            acc[span(0, 4)] += middle[: POS // 4]
            acc[span(12, 4)] += middle[POS // 4 :]
            acc[span(4, 4)] += back2(0, 4, 0, half)
            acc[span(8, 4)] += back2(12, 4, 2, half)

    def inner_back2(half):
        acc[span(4, 8)] += back2(4, 8, 1, half)
        acc[span(0, 8)] += back2(4, 8, 2, half)
        acc[span(8, 8)] += back2(4, 8, 0, half)

    cotangent(0)
    inner_back2(0)
    for half in (0, 1):
        wait_halo(cot_halo[half])
        take_halo(grad2, 2 + half, 4, LANES[half])
        acc[span(0, 4)] += back2(-4, 4, 0, half)
        acc[span(12, 4)] += back2(16, 4, 2, half)
    cotangent(1)
    inner_back2(1)

    def grad1_rows(first, count):
        @pl.loop(0, count // 2)
        def _(i):
            source = pl.ds(pl.multiple_of((first + i * 2) * COLS, 2 * COLS), 2 * COLS)
            at = pl.ds(pl.multiple_of((first + i * 2 + 2) * COLS, 2 * COLS), 2 * COLS)
            value = acc[source, :] * pre1[source, :]
            grad1[1, at, :] = value.astype(BF16)
            put_shifted(grad1, at, value, 2)

    grad1_rows(0, 2)
    grad1_rows(ROWS - 2, 2)
    hid_grad_halo = halo_copies(4, grad1.at[1, span(2, 2)], grad1.at[1, span(ROWS, 2)])
    grad1_rows(2, ROWS - 4)

    def back1(first, count, a):
        return sum(
            mul_t(grad1[b, span(first + 2, count)], w1[2 - a, 2 - b]) for b in range(TAPS)
        )

    acc[...] = back1(0, ROWS, 1)
    acc[span(2, ROWS - 2)] += back1(0, ROWS - 2, 0)
    acc[span(0, ROWS - 2)] += back1(2, ROWS - 2, 2)
    out[0, 2 : ROWS - 2] = acc[span(2, ROWS - 4)].reshape(ROWS - 4, COLS, CH).astype(BF16)
    wait_halo(hid_grad_halo)
    take_halo(grad1, 4, 2)
    out[0, 0:2] = (acc[span(0, 2)] + back1(-2, 2, 0)).reshape(2, COLS, CH).astype(BF16)
    out[0, ROWS - 2 :] = (
        (acc[span(ROWS - 2, 2)] + back1(ROWS, 2, 2)).reshape(2, COLS, CH).astype(BF16)
    )

    for down, up in (image_halo, hidden_halo, *cot_halo, hid_grad_halo):

        @pl.when(has_after)
        def _(down=down):
            down.wait_send()

        @pl.when(has_before)
        def _(up=up):
            up.wait_send()

    for phase, source, landing in ((0, feat, spread), (1, picked, partner)):
        for chunk in range(4):
            for i in range(PEERS):
                swap_copy(chunk, phase, source, landing, i, peer).wait_send()


def per_device(*args):
    hbm = pl.BlockSpec(memory_space=pltpu.HBM)
    vmem = pl.BlockSpec(memory_space=pltpu.VMEM)
    dma = pltpu.SemaphoreType.DMA
    pieces = pltpu.VMEM((PEERS, COLS, HALF), BF16)
    return pl.pallas_call(
        kernel,
        out_shape=jax.ShapeDtypeStruct((1, ROWS, COLS, CH), BF16),
        in_specs=[hbm] * 9,
        out_specs=vmem,
        scratch_shapes=[
            pltpu.SMEM((PEERS,), jnp.int32),
            pltpu.VMEM((4, 1, CH), F32),
            pltpu.VMEM((TAPS, TAPS, CH, CH), BF16),
            pltpu.VMEM((TAPS, TAPS, CH, CH), BF16),
            pltpu.VMEM((TAPS, (ROWS + 4) * COLS, CH), BF16),
            pltpu.VMEM((TAPS, (ROWS + 8) * COLS, CH), BF16),
            pltpu.VMEM((TAPS, (ROWS + 8) * COLS, CH), BF16),
            pltpu.VMEM((TAPS, (ROWS + 4) * COLS, CH), BF16),
            pltpu.VMEM((2, 2 * COLS, CH), BF16),
            pltpu.VMEM((2, 4 * COLS, CH), BF16),
            pltpu.VMEM((2, 4 * COLS, HALF), BF16),
            pltpu.VMEM((2, 4 * COLS, HALF), BF16),
            pltpu.VMEM((2, 2 * COLS, CH), BF16),
            pltpu.VMEM((POS, CH), F32),
            pltpu.VMEM((POS, CH), F32),
            pltpu.VMEM((POS, CH), F32),
            pltpu.VMEM((ROWS, COLS, CH), BF16),
            *[pieces] * 16,
            dma((7,)),
            dma((TAPS,)),
            dma((TAPS,)),
            dma((5, 2)),
            dma((5, 2)),
            dma((4, 2, PEERS)),
            dma((4, 2, PEERS)),
        ],
        compiler_params=pltpu.CompilerParams(
            collective_id=0, has_side_effects=True, vmem_limit_bytes=34 << 20
        ),
        name="distill",
    )(
        *(
            pltpu.with_memory_space_constraint(x, pltpu.HBM)
            for x in (args[2], args[0].reshape(1, POS, CH), args[1], *args[3:])
        )
    )


def solution(mesh):
    placed = (
        P("peer", "space", None, None),
        P("peer", "space", None, None),
        P(),
        P("peer", None, None, None, None),
        P("peer", None),
        P("peer", None),
        P("peer", None, None, None, None),
        P("peer", None),
        P("peer", None),
    )
    return jax.shard_map(
        per_device,
        mesh=mesh,
        in_specs=placed,
        out_specs=P("peer", "space", None, None),
        check_vma=False,
    )
```

```python
import jax
import jax.numpy as jnp
from jax import lax
from jax.experimental import pallas as pl
from jax.experimental.pallas import tpu as pltpu
from jax.sharding import PartitionSpec as P

MESH = pl.DeviceIdType.MESH
BF16 = jnp.bfloat16
F32 = jnp.float32

ROWS = 16
COLS = 32
CH = 512
PEERS = 8
SPACE = 32
TAPS = 3
POS = ROWS * COLS
HALF = CH // 2
EDGE = (0, 1, 2, 3, 12, 13, 14, 15)
INNER = tuple(range(4, 12))
LANES = (pl.ds(0, HALF), pl.ds(HALF, HALF))
CHUNKS = ((INNER, 0), (INNER, 1), (EDGE, 0), (EDGE, 1))


def sigmoid(value):
    return 0.5 + 0.5 * jnp.tanh(0.5 * value)


def span(first, count):
    return pl.ds(first * COLS, count * COLS)


def mul(left, right):
    return jnp.dot(left, right, preferred_element_type=F32)


def mul_t(left, right):
    return lax.dot_general(left, right, (((1,), (1,)), ((), ())), preferred_element_type=F32)


def put_shifted(buf, at, value, step, lanes=slice(None)):
    count = value.shape[0]
    col = lax.broadcasted_iota(jnp.int32, value.shape, 0) & (COLS - 1)
    ahead = jnp.where(col >= step, pltpu.roll(value, step, 0), 0.0)
    behind = jnp.where(col < COLS - step, pltpu.roll(value, count - step, 0), 0.0)
    buf[0, at, lanes] = ahead.astype(BF16)
    buf[2, at, lanes] = behind.astype(BF16)


def kernel(
    pairing_in,
    images,
    task_grad,
    first_kernel,
    first_scale,
    first_shift,
    second_kernel,
    second_scale,
    second_shift,
    out,
    pairing,
    norms,
    w1,
    w2,
    img,
    hid,
    grad2,
    grad1,
    img_halo,
    hid_halo,
    grad2_halo_a,
    grad2_halo_b,
    grad1_halo,
    pre1,
    pre2,
    acc,
    task,
    *rest,
):
    feat, spread, picked, partner = (rest[4 * i : 4 * i + 4] for i in range(4))
    load_sem, w1_sem, w2_sem, halo_send, halo_recv, swap_send, swap_recv = rest[16:]
    peer = lax.axis_index("peer")
    place = lax.axis_index("space")
    across = lax.rem(place + SPACE // 2, SPACE)
    after = lax.rem(place + 1, SPACE)
    before = lax.rem(place + SPACE - 1, SPACE)
    has_after = place < SPACE - 1
    has_before = place > 0

    image_load = pltpu.make_async_copy(images.at[0], img.at[1, span(2, ROWS)], load_sem.at[0])
    image_load.start()
    w1_loads = [
        pltpu.make_async_copy(first_kernel.at[0, a], w1.at[a], w1_sem.at[a]) for a in range(TAPS)
    ]
    w2_loads = [
        pltpu.make_async_copy(second_kernel.at[0, a], w2.at[a], w2_sem.at[a]) for a in range(TAPS)
    ]
    task_load = pltpu.make_async_copy(task_grad.at[0], task, load_sem.at[1])
    for a in (1, 0, 2):
        w1_loads[a].start()
    small_loads = [
        pltpu.make_async_copy(array, norms.at[i], load_sem.at[2 + i])
        for i, array in enumerate((first_scale, first_shift, second_scale, second_shift))
    ]
    small_loads.append(pltpu.make_async_copy(pairing_in, pairing, load_sem.at[6]))
    for load in small_loads:
        load.start()

    barrier = pltpu.get_barrier_semaphore()
    for neighbour in (before, after):
        pl.semaphore_signal(barrier, inc=1, device_id=(peer, neighbour), device_id_type=MESH)
    for other in range(PEERS):
        pl.semaphore_signal(barrier, inc=1, device_id=(other, across), device_id_type=MESH)

    landings = (img_halo, hid_halo, grad2_halo_a, grad2_halo_b, grad1_halo)
    for side, missing in ((0, place == 0), (1, place == SPACE - 1)):

        @pl.when(missing)
        def _(side=side):
            for landing in landings:
                landing[side] = jnp.zeros(landing.shape[1:], BF16)

    pl.semaphore_wait(barrier, 2 + PEERS)

    def halo_copies(stage, head, tail):
        down = pltpu.make_async_remote_copy(
            src_ref=tail,
            dst_ref=landings[stage].at[0],
            send_sem=halo_send.at[stage, 0],
            recv_sem=halo_recv.at[stage, 0],
            device_id=(peer, after),
            device_id_type=MESH,
        )
        up = pltpu.make_async_remote_copy(
            src_ref=head,
            dst_ref=landings[stage].at[1],
            send_sem=halo_send.at[stage, 1],
            recv_sem=halo_recv.at[stage, 1],
            device_id=(peer, before),
            device_id_type=MESH,
        )

        @pl.when(has_after)
        def _():
            down.start()

        @pl.when(has_before)
        def _():
            up.start()

        return down, up

    def wait_halo(copies):
        down, up = copies

        @pl.when(has_before)
        def _():
            down.wait_recv()

        @pl.when(has_after)
        def _():
            up.wait_recv()

    def take_halo(buf, stage, step, lanes=slice(None)):
        for side in (0, 1):
            at = span(0 if side == 0 else ROWS + step, step)
            value = landings[stage][side]
            buf[1, at, lanes] = value
            put_shifted(buf, at, value.astype(F32), step, lanes)

    def swap_copy(chunk, phase, source, landing, i, slot):
        return pltpu.make_async_remote_copy(
            src_ref=source[chunk].at[i],
            dst_ref=landing[chunk].at[slot],
            send_sem=swap_send.at[chunk, phase, i],
            recv_sem=swap_recv.at[chunk, phase, slot],
            device_id=(i, across),
            device_id_type=MESH,
        )

    def send_pieces(chunk, phase):
        source, landing = ((feat, spread), (picked, partner))[phase]
        for i in range(PEERS):
            swap_copy(chunk, phase, source, landing, i, peer).start()

    def wait_pieces(chunk, phase):
        source, landing = ((feat, spread), (picked, partner))[phase]
        for i in range(PEERS):
            swap_copy(chunk, phase, source, landing, i, i).wait_recv()

    image_halo = halo_copies(0, images.at[0, span(0, 2)], images.at[0, span(ROWS - 2, 2)])

    image_load.wait()

    @pl.loop(0, ROWS // 2, unroll=True)
    def _(i):
        at = pl.ds(pl.multiple_of((i * 2 + 2) * COLS, 2 * COLS), 2 * COLS)
        put_shifted(img, at, img[1, at, :].astype(F32), 2)

    w1_loads[1].wait()
    acc[...] = sum(mul(img[b, span(2, ROWS)], w1[1, b]) for b in range(TAPS))
    for load in w2_loads:
        load.start()
    task_load.start()
    w1_loads[0].wait()
    acc[span(2, ROWS - 2)] += sum(mul(img[b, span(2, ROWS - 2)], w1[0, b]) for b in range(TAPS))
    w1_loads[2].wait()
    acc[span(0, ROWS - 2)] += sum(mul(img[b, span(4, ROWS - 2)], w1[2, b]) for b in range(TAPS))

    for load in small_loads:
        load.wait()
    scale1, shift1, scale2, shift2 = (norms[i] for i in range(4))

    def hidden_rows(first, count):
        @pl.loop(0, count // 2, unroll=True)
        def _(i):
            source = pl.ds(pl.multiple_of((first + i * 2) * COLS, 2 * COLS), 2 * COLS)
            at = pl.ds(pl.multiple_of((first + i * 2 + 4) * COLS, 2 * COLS), 2 * COLS)
            value = scale1 * acc[source, :] + shift1
            pre1[source, :] = value
            value = value * sigmoid(value)
            hid[1, at, :] = value.astype(BF16)
            put_shifted(hid, at, value, 4)

    hidden_rows(4, 8)
    wait_halo(image_halo)
    take_halo(img, 0, 2)
    acc[span(0, 2)] += sum(mul(img[b, span(0, 2)], w1[0, b]) for b in range(TAPS))
    acc[span(ROWS - 2, 2)] += sum(mul(img[b, span(ROWS + 2, 2)], w1[2, b]) for b in range(TAPS))
    hidden_rows(0, 4)
    hidden_rows(12, 4)
    hidden_halo = halo_copies(1, hid.at[1, span(4, 4)], hid.at[1, span(ROWS, 4)])

    for load in w2_loads:
        load.wait()

    def features(chunk):
        rows, half = CHUNKS[chunk]
        lanes = LANES[half]
        scale = scale2[:, half * HALF : (half + 1) * HALF]
        shift = shift2[:, half * HALF : (half + 1) * HALF]
        for i, row in enumerate(rows):
            at = span(row, 1)
            value = scale * acc[at, lanes] + shift
            pre2[at, lanes] = value
            feat[chunk][i] = (value * sigmoid(value)).astype(BF16)
        send_pieces(chunk, 0)

    for half in (0, 1):
        acc[span(4, 8), LANES[half]] = sum(
            mul(hid[b, span(4 + 4 * a, 8)], w2[a, b, :, LANES[half]])
            for a in range(TAPS)
            for b in range(TAPS)
        )
        features(half)

    middle = sum(
        mul(jnp.concatenate([hid[b, span(4, 4)], hid[b, span(16, 4)]], 0), w2[1, b])
        for b in range(TAPS)
    )
    acc[span(0, 4)] = middle[: POS // 4]
    acc[span(12, 4)] = middle[POS // 4 :]
    acc[span(0, 4)] += sum(mul(hid[b, span(8, 4)], w2[2, b]) for b in range(TAPS))
    acc[span(12, 4)] += sum(mul(hid[b, span(12, 4)], w2[0, b]) for b in range(TAPS))
    wait_halo(hidden_halo)
    take_halo(hid, 1, 4)
    for half in (0, 1):
        for row, at, a in ((0, 0, 0), (12, 20, 2)):
            acc[span(row, 4), LANES[half]] += sum(
                mul(hid[b, span(at, 4)], w2[a, b, :, LANES[half]]) for b in range(TAPS)
            )
        features(2 + half)

    def slope(value):
        s = sigmoid(value)
        return s * (1.0 + value * (1.0 - s))

    @pl.loop(0, ROWS)
    def _(i):
        at = pl.ds(pl.multiple_of(i * COLS, COLS), COLS)
        pre2[at, :] = slope(pre2[at, :]) * scale2
        pre1[at, :] = slope(pre1[at, :]) * scale1

    task_load.wait()

    def pass_on(chunk):
        wait_pieces(chunk, 0)
        for i in range(PEERS):
            picked[chunk][i] = spread[chunk][pairing[i]]
        send_pieces(chunk, 1)

    for chunk in (2, 3, 0, 1):
        pass_on(chunk)

    def cotangent(chunk):
        rows, half = CHUNKS[chunk]
        lanes = LANES[half]
        wait_pieces(chunk, 1)
        for i, row in enumerate(rows):
            cot = task[row, :, lanes].astype(F32) + feat[chunk][i].astype(F32)
            value = (cot - partner[chunk][i].astype(F32)) * pre2[span(row, 1), lanes]
            to = span(row + 4, 1)
            grad2[1, to, lanes] = value.astype(BF16)
            put_shifted(grad2, to, value, 4, lanes)

    def back2(first, count, a, half):
        lanes = LANES[half]
        return sum(
            mul_t(grad2[b, span(first + 4, count), lanes], w2[2 - a, 2 - b, :, lanes])
            for b in range(TAPS)
        )

    cot_halo = []
    for half in (0, 1):
        lanes = LANES[half]
        cotangent(2 + half)
        cot_halo.append(
            halo_copies(
                2 + half, grad2.at[1, span(4, 4), lanes], grad2.at[1, span(ROWS, 4), lanes]
            )
        )
        middle = sum(
            mul_t(
                jnp.concatenate([grad2[b, span(4, 4), lanes], grad2[b, span(16, 4), lanes]], 0),
                w2[1, 2 - b, :, lanes],
            )
            for b in range(TAPS)
        )
        if half == 0:
            acc[span(0, 4)] = middle[: POS // 4]
            acc[span(12, 4)] = middle[POS // 4 :]
            acc[span(4, 4)] = back2(0, 4, 0, half)
            acc[span(8, 4)] = back2(12, 4, 2, half)
        else:
            acc[span(0, 4)] += middle[: POS // 4]
            acc[span(12, 4)] += middle[POS // 4 :]
            acc[span(4, 4)] += back2(0, 4, 0, half)
            acc[span(8, 4)] += back2(12, 4, 2, half)

    def inner_back2(half):
        acc[span(4, 8)] += back2(4, 8, 1, half)
        acc[span(0, 8)] += back2(4, 8, 2, half)
        acc[span(8, 8)] += back2(4, 8, 0, half)

    cotangent(0)
    inner_back2(0)
    cotangent(1)
    inner_back2(1)
    for half in (0, 1):
        wait_halo(cot_halo[half])
        take_halo(grad2, 2 + half, 4, LANES[half])
        acc[span(0, 4)] += back2(-4, 4, 0, half)
        acc[span(12, 4)] += back2(16, 4, 2, half)

    def grad1_rows(first, count):
        @pl.loop(0, count // 2, unroll=True)
        def _(i):
            source = pl.ds(pl.multiple_of((first + i * 2) * COLS, 2 * COLS), 2 * COLS)
            at = pl.ds(pl.multiple_of((first + i * 2 + 2) * COLS, 2 * COLS), 2 * COLS)
            value = acc[source, :] * pre1[source, :]
            grad1[1, at, :] = value.astype(BF16)
            put_shifted(grad1, at, value, 2)

    grad1_rows(0, 2)
    grad1_rows(ROWS - 2, 2)
    hid_grad_halo = halo_copies(4, grad1.at[1, span(2, 2)], grad1.at[1, span(ROWS, 2)])
    grad1_rows(2, ROWS - 4)

    def back1(first, count, a):
        return sum(
            mul_t(grad1[b, span(first + 2, count)], w1[2 - a, 2 - b]) for b in range(TAPS)
        )

    acc[...] = back1(0, ROWS, 1)
    acc[span(2, ROWS - 2)] += back1(0, ROWS - 2, 0)
    acc[span(0, ROWS - 2)] += back1(2, ROWS - 2, 2)
    out[0, 2 : ROWS - 2] = acc[span(2, ROWS - 4)].reshape(ROWS - 4, COLS, CH).astype(BF16)
    wait_halo(hid_grad_halo)
    take_halo(grad1, 4, 2)
    out[0, 0:2] = (acc[span(0, 2)] + back1(-2, 2, 0)).reshape(2, COLS, CH).astype(BF16)
    out[0, ROWS - 2 :] = (
        (acc[span(ROWS - 2, 2)] + back1(ROWS, 2, 2)).reshape(2, COLS, CH).astype(BF16)
    )

    for down, up in (image_halo, hidden_halo, *cot_halo, hid_grad_halo):

        @pl.when(has_after)
        def _(down=down):
            down.wait_send()

        @pl.when(has_before)
        def _(up=up):
            up.wait_send()

    for phase, source, landing in ((0, feat, spread), (1, picked, partner)):
        for chunk in range(4):
            for i in range(PEERS):
                swap_copy(chunk, phase, source, landing, i, peer).wait_send()


def per_device(*args):
    hbm = pl.BlockSpec(memory_space=pltpu.HBM)
    vmem = pl.BlockSpec(memory_space=pltpu.VMEM)
    dma = pltpu.SemaphoreType.DMA
    pieces = pltpu.VMEM((PEERS, COLS, HALF), BF16)
    return pl.pallas_call(
        kernel,
        out_shape=jax.ShapeDtypeStruct((1, ROWS, COLS, CH), BF16),
        in_specs=[hbm] * 9,
        out_specs=vmem,
        scratch_shapes=[
            pltpu.SMEM((PEERS,), jnp.int32),
            pltpu.VMEM((4, 1, CH), F32),
            pltpu.VMEM((TAPS, TAPS, CH, CH), BF16),
            pltpu.VMEM((TAPS, TAPS, CH, CH), BF16),
            pltpu.VMEM((TAPS, (ROWS + 4) * COLS, CH), BF16),
            pltpu.VMEM((TAPS, (ROWS + 8) * COLS, CH), BF16),
            pltpu.VMEM((TAPS, (ROWS + 8) * COLS, CH), BF16),
            pltpu.VMEM((TAPS, (ROWS + 4) * COLS, CH), BF16),
            pltpu.VMEM((2, 2 * COLS, CH), BF16),
            pltpu.VMEM((2, 4 * COLS, CH), BF16),
            pltpu.VMEM((2, 4 * COLS, HALF), BF16),
            pltpu.VMEM((2, 4 * COLS, HALF), BF16),
            pltpu.VMEM((2, 2 * COLS, CH), BF16),
            pltpu.VMEM((POS, CH), F32),
            pltpu.VMEM((POS, CH), F32),
            pltpu.VMEM((POS, CH), F32),
            pltpu.VMEM((ROWS, COLS, CH), BF16),
            *[pieces] * 16,
            dma((7,)),
            dma((TAPS,)),
            dma((TAPS,)),
            dma((5, 2)),
            dma((5, 2)),
            dma((4, 2, PEERS)),
            dma((4, 2, PEERS)),
        ],
        compiler_params=pltpu.CompilerParams(
            collective_id=0, has_side_effects=True, vmem_limit_bytes=34 << 20
        ),
        name="distill",
    )(
        *(
            pltpu.with_memory_space_constraint(x, pltpu.HBM)
            for x in (args[2], args[0].reshape(1, POS, CH), args[1], *args[3:])
        )
    )


def solution(mesh):
    placed = (
        P("peer", "space", None, None),
        P("peer", "space", None, None),
        P(),
        P("peer", None, None, None, None),
        P("peer", None),
        P("peer", None),
        P("peer", None, None, None, None),
        P("peer", None),
        P("peer", None),
    )
    return jax.shard_map(
        per_device,
        mesh=mesh,
        in_specs=placed,
        out_specs=P("peer", "space", None, None),
        check_vma=False,
    )
```

```python
import jax
import jax.numpy as jnp
from jax import lax
from jax.experimental import pallas as pl
from jax.experimental.pallas import tpu as pltpu
from jax.sharding import PartitionSpec as P

MESH = pl.DeviceIdType.MESH
BF16 = jnp.bfloat16
F32 = jnp.float32

ROWS = 16
COLS = 32
CH = 512
PEERS = 8
SPACE = 32
TAPS = 3
POS = ROWS * COLS
HALF = CH // 2
EDGE = (0, 1, 2, 3, 12, 13, 14, 15)
INNER = tuple(range(4, 12))
LANES = (pl.ds(0, HALF), pl.ds(HALF, HALF))
CHUNKS = ((INNER, 0), (INNER, 1), (EDGE, 0), (EDGE, 1))


def sigmoid(value):
    return 0.5 + 0.5 * jnp.tanh(0.5 * value)


def span(first, count):
    return pl.ds(first * COLS, count * COLS)


def mul(left, right):
    return jnp.dot(left, right, preferred_element_type=F32)


def mul_t(left, right):
    return lax.dot_general(left, right, (((1,), (1,)), ((), ())), preferred_element_type=F32)


def put_shifted(buf, at, value, step, lanes=slice(None)):
    count = value.shape[0]
    col = lax.broadcasted_iota(jnp.int32, value.shape, 0) & (COLS - 1)
    ahead = jnp.where(col >= step, pltpu.roll(value, step, 0), 0.0)
    behind = jnp.where(col < COLS - step, pltpu.roll(value, count - step, 0), 0.0)
    buf[0, at, lanes] = ahead.astype(BF16)
    buf[2, at, lanes] = behind.astype(BF16)


def kernel(
    pairing_in,
    images,
    task_grad,
    first_kernel,
    first_scale,
    first_shift,
    second_kernel,
    second_scale,
    second_shift,
    out,
    pairing,
    norms,
    w1,
    w2,
    img,
    hid,
    grad2,
    grad1,
    img_halo,
    hid_halo,
    grad2_halo_a,
    grad2_halo_b,
    grad1_halo,
    pre1,
    pre2,
    acc,
    task,
    *rest,
):
    feat, spread, picked, partner = (rest[4 * i : 4 * i + 4] for i in range(4))
    load_sem, w1_sem, w2_sem, halo_send, halo_recv, swap_send, swap_recv = rest[16:]
    peer = lax.axis_index("peer")
    place = lax.axis_index("space")
    across = lax.rem(place + SPACE // 2, SPACE)
    after = lax.rem(place + 1, SPACE)
    before = lax.rem(place + SPACE - 1, SPACE)
    has_after = place < SPACE - 1
    has_before = place > 0

    image_load = pltpu.make_async_copy(images.at[0], img.at[1, span(2, ROWS)], load_sem.at[0])
    image_load.start()
    w1_loads = [
        pltpu.make_async_copy(first_kernel.at[0, a], w1.at[a], w1_sem.at[a]) for a in range(TAPS)
    ]
    w2_loads = [
        pltpu.make_async_copy(second_kernel.at[0, a], w2.at[a], w2_sem.at[a]) for a in range(TAPS)
    ]
    task_load = pltpu.make_async_copy(task_grad.at[0], task, load_sem.at[1])
    for a in (1, 0, 2):
        w1_loads[a].start()
    small_loads = [
        pltpu.make_async_copy(array, norms.at[i], load_sem.at[2 + i])
        for i, array in enumerate((first_scale, first_shift, second_scale, second_shift))
    ]
    small_loads.append(pltpu.make_async_copy(pairing_in, pairing, load_sem.at[6]))
    for load in small_loads:
        load.start()

    barrier = pltpu.get_barrier_semaphore()
    for neighbour in (before, after):
        pl.semaphore_signal(barrier, inc=1, device_id=(peer, neighbour), device_id_type=MESH)
    for other in range(PEERS):
        pl.semaphore_signal(barrier, inc=1, device_id=(other, across), device_id_type=MESH)

    landings = (img_halo, hid_halo, grad2_halo_a, grad2_halo_b, grad1_halo)
    for side, missing in ((0, place == 0), (1, place == SPACE - 1)):

        @pl.when(missing)
        def _(side=side):
            for landing in landings:
                landing[side] = jnp.zeros(landing.shape[1:], BF16)

    pl.semaphore_wait(barrier, 2 + PEERS)

    def halo_copies(stage, head, tail):
        down = pltpu.make_async_remote_copy(
            src_ref=tail,
            dst_ref=landings[stage].at[0],
            send_sem=halo_send.at[stage, 0],
            recv_sem=halo_recv.at[stage, 0],
            device_id=(peer, after),
            device_id_type=MESH,
        )
        up = pltpu.make_async_remote_copy(
            src_ref=head,
            dst_ref=landings[stage].at[1],
            send_sem=halo_send.at[stage, 1],
            recv_sem=halo_recv.at[stage, 1],
            device_id=(peer, before),
            device_id_type=MESH,
        )

        @pl.when(has_after)
        def _():
            down.start()

        @pl.when(has_before)
        def _():
            up.start()

        return down, up

    def wait_halo(copies):
        down, up = copies

        @pl.when(has_before)
        def _():
            down.wait_recv()

        @pl.when(has_after)
        def _():
            up.wait_recv()

    def take_halo(buf, stage, step, lanes=slice(None)):
        for side in (0, 1):
            at = span(0 if side == 0 else ROWS + step, step)
            value = landings[stage][side]
            buf[1, at, lanes] = value
            put_shifted(buf, at, value.astype(F32), step, lanes)

    def swap_copy(chunk, phase, source, landing, i, slot):
        return pltpu.make_async_remote_copy(
            src_ref=source[chunk].at[i],
            dst_ref=landing[chunk].at[slot],
            send_sem=swap_send.at[chunk, phase, i],
            recv_sem=swap_recv.at[chunk, phase, slot],
            device_id=(i, across),
            device_id_type=MESH,
        )

    def send_pieces(chunk, phase):
        source, landing = ((feat, spread), (picked, partner))[phase]
        for i in range(PEERS):
            swap_copy(chunk, phase, source, landing, i, peer).start()

    def wait_pieces(chunk, phase):
        source, landing = ((feat, spread), (picked, partner))[phase]
        for i in range(PEERS):
            swap_copy(chunk, phase, source, landing, i, i).wait_recv()

    image_halo = halo_copies(0, images.at[0, span(0, 2)], images.at[0, span(ROWS - 2, 2)])

    image_load.wait()

    @pl.loop(0, ROWS // 2, unroll=True)
    def _(i):
        at = pl.ds(pl.multiple_of((i * 2 + 2) * COLS, 2 * COLS), 2 * COLS)
        put_shifted(img, at, img[1, at, :].astype(F32), 2)

    w1_loads[1].wait()
    acc[...] = sum(mul(img[b, span(2, ROWS)], w1[1, b]) for b in range(TAPS))
    for load in w2_loads:
        load.start()
    task_load.start()
    w1_loads[0].wait()
    acc[span(2, ROWS - 2)] += sum(mul(img[b, span(2, ROWS - 2)], w1[0, b]) for b in range(TAPS))
    w1_loads[2].wait()
    acc[span(0, ROWS - 2)] += sum(mul(img[b, span(4, ROWS - 2)], w1[2, b]) for b in range(TAPS))

    for load in small_loads:
        load.wait()
    scale1, shift1, scale2, shift2 = (norms[i] for i in range(4))

    def hidden_rows(first, count):
        @pl.loop(0, count // 2, unroll=True)
        def _(i):
            source = pl.ds(pl.multiple_of((first + i * 2) * COLS, 2 * COLS), 2 * COLS)
            at = pl.ds(pl.multiple_of((first + i * 2 + 4) * COLS, 2 * COLS), 2 * COLS)
            value = scale1 * acc[source, :] + shift1
            pre1[source, :] = value
            value = value * sigmoid(value)
            hid[1, at, :] = value.astype(BF16)
            put_shifted(hid, at, value, 4)

    hidden_rows(4, 8)
    wait_halo(image_halo)
    take_halo(img, 0, 2)
    acc[span(0, 2)] += sum(mul(img[b, span(0, 2)], w1[0, b]) for b in range(TAPS))
    acc[span(ROWS - 2, 2)] += sum(mul(img[b, span(ROWS + 2, 2)], w1[2, b]) for b in range(TAPS))
    hidden_rows(0, 4)
    hidden_rows(12, 4)
    hidden_halo = halo_copies(1, hid.at[1, span(4, 4)], hid.at[1, span(ROWS, 4)])

    for load in w2_loads:
        load.wait()

    def features(chunk):
        rows, half = CHUNKS[chunk]
        lanes = LANES[half]
        scale = scale2[:, half * HALF : (half + 1) * HALF]
        shift = shift2[:, half * HALF : (half + 1) * HALF]
        for i, row in enumerate(rows):
            at = span(row, 1)
            value = scale * acc[at, lanes] + shift
            pre2[at, lanes] = value
            feat[chunk][i] = (value * sigmoid(value)).astype(BF16)
        send_pieces(chunk, 0)

    for half in (0, 1):
        acc[span(4, 8), LANES[half]] = sum(
            mul(hid[b, span(4 + 4 * a, 8)], w2[a, b, :, LANES[half]])
            for a in range(TAPS)
            for b in range(TAPS)
        )
        features(half)

    middle = sum(
        mul(jnp.concatenate([hid[b, span(4, 4)], hid[b, span(16, 4)]], 0), w2[1, b])
        for b in range(TAPS)
    )
    acc[span(0, 4)] = middle[: POS // 4]
    acc[span(12, 4)] = middle[POS // 4 :]
    acc[span(0, 4)] += sum(mul(hid[b, span(8, 4)], w2[2, b]) for b in range(TAPS))
    acc[span(12, 4)] += sum(mul(hid[b, span(12, 4)], w2[0, b]) for b in range(TAPS))
    wait_halo(hidden_halo)
    take_halo(hid, 1, 4)
    for half in (0, 1):
        for row, at, a in ((0, 0, 0), (12, 20, 2)):
            acc[span(row, 4), LANES[half]] += sum(
                mul(hid[b, span(at, 4)], w2[a, b, :, LANES[half]]) for b in range(TAPS)
            )
        features(2 + half)

    def slope(value):
        s = sigmoid(value)
        return s * (1.0 + value * (1.0 - s))

    @pl.loop(0, ROWS)
    def _(i):
        at = pl.ds(pl.multiple_of(i * COLS, COLS), COLS)
        pre2[at, :] = slope(pre2[at, :]) * scale2
        pre1[at, :] = slope(pre1[at, :]) * scale1

    task_load.wait()

    def pass_on(chunk):
        wait_pieces(chunk, 0)
        for i in range(PEERS):
            picked[chunk][i] = spread[chunk][pairing[i]]
        send_pieces(chunk, 1)

    for chunk in (0, 2, 3, 1):
        pass_on(chunk)

    def cotangent(chunk):
        rows, half = CHUNKS[chunk]
        lanes = LANES[half]
        wait_pieces(chunk, 1)
        for i, row in enumerate(rows):
            cot = task[row, :, lanes].astype(F32) + feat[chunk][i].astype(F32)
            value = (cot - partner[chunk][i].astype(F32)) * pre2[span(row, 1), lanes]
            to = span(row + 4, 1)
            grad2[1, to, lanes] = value.astype(BF16)
            put_shifted(grad2, to, value, 4, lanes)

    def back2(first, count, a, half):
        lanes = LANES[half]
        return sum(
            mul_t(grad2[b, span(first + 4, count), lanes], w2[2 - a, 2 - b, :, lanes])
            for b in range(TAPS)
        )

    cot_halo = []
    for half in (0, 1):
        lanes = LANES[half]
        cotangent(2 + half)
        cot_halo.append(
            halo_copies(
                2 + half, grad2.at[1, span(4, 4), lanes], grad2.at[1, span(ROWS, 4), lanes]
            )
        )
        middle = sum(
            mul_t(
                jnp.concatenate([grad2[b, span(4, 4), lanes], grad2[b, span(16, 4), lanes]], 0),
                w2[1, 2 - b, :, lanes],
            )
            for b in range(TAPS)
        )
        if half == 0:
            acc[span(0, 4)] = middle[: POS // 4]
            acc[span(12, 4)] = middle[POS // 4 :]
            acc[span(4, 4)] = back2(0, 4, 0, half)
            acc[span(8, 4)] = back2(12, 4, 2, half)
        else:
            acc[span(0, 4)] += middle[: POS // 4]
            acc[span(12, 4)] += middle[POS // 4 :]
            acc[span(4, 4)] += back2(0, 4, 0, half)
            acc[span(8, 4)] += back2(12, 4, 2, half)

    def inner_back2(half):
        acc[span(4, 8)] += back2(4, 8, 1, half)
        acc[span(0, 8)] += back2(4, 8, 2, half)
        acc[span(8, 8)] += back2(4, 8, 0, half)

    cotangent(0)
    inner_back2(0)
    cotangent(1)
    inner_back2(1)
    for half in (0, 1):
        wait_halo(cot_halo[half])
        take_halo(grad2, 2 + half, 4, LANES[half])
        acc[span(0, 4)] += back2(-4, 4, 0, half)
        acc[span(12, 4)] += back2(16, 4, 2, half)

    def grad1_rows(first, count):
        @pl.loop(0, count // 2, unroll=True)
        def _(i):
            source = pl.ds(pl.multiple_of((first + i * 2) * COLS, 2 * COLS), 2 * COLS)
            at = pl.ds(pl.multiple_of((first + i * 2 + 2) * COLS, 2 * COLS), 2 * COLS)
            value = acc[source, :] * pre1[source, :]
            grad1[1, at, :] = value.astype(BF16)
            put_shifted(grad1, at, value, 2)

    grad1_rows(0, 2)
    grad1_rows(ROWS - 2, 2)
    hid_grad_halo = halo_copies(4, grad1.at[1, span(2, 2)], grad1.at[1, span(ROWS, 2)])
    grad1_rows(2, ROWS - 4)

    def back1(first, count, a):
        return sum(
            mul_t(grad1[b, span(first + 2, count)], w1[2 - a, 2 - b]) for b in range(TAPS)
        )

    acc[...] = back1(0, ROWS, 1)
    acc[span(2, ROWS - 2)] += back1(0, ROWS - 2, 0)
    acc[span(0, ROWS - 2)] += back1(2, ROWS - 2, 2)
    out[0, 2 : ROWS - 2] = acc[span(2, ROWS - 4)].reshape(ROWS - 4, COLS, CH).astype(BF16)
    wait_halo(hid_grad_halo)
    take_halo(grad1, 4, 2)
    out[0, 0:2] = (acc[span(0, 2)] + back1(-2, 2, 0)).reshape(2, COLS, CH).astype(BF16)
    out[0, ROWS - 2 :] = (
        (acc[span(ROWS - 2, 2)] + back1(ROWS, 2, 2)).reshape(2, COLS, CH).astype(BF16)
    )

    for down, up in (image_halo, hidden_halo, *cot_halo, hid_grad_halo):

        @pl.when(has_after)
        def _(down=down):
            down.wait_send()

        @pl.when(has_before)
        def _(up=up):
            up.wait_send()

    for phase, source, landing in ((0, feat, spread), (1, picked, partner)):
        for chunk in range(4):
            for i in range(PEERS):
                swap_copy(chunk, phase, source, landing, i, peer).wait_send()


def per_device(*args):
    hbm = pl.BlockSpec(memory_space=pltpu.HBM)
    vmem = pl.BlockSpec(memory_space=pltpu.VMEM)
    dma = pltpu.SemaphoreType.DMA
    pieces = pltpu.VMEM((PEERS, COLS, HALF), BF16)
    return pl.pallas_call(
        kernel,
        out_shape=jax.ShapeDtypeStruct((1, ROWS, COLS, CH), BF16),
        in_specs=[hbm] * 9,
        out_specs=vmem,
        scratch_shapes=[
            pltpu.SMEM((PEERS,), jnp.int32),
            pltpu.VMEM((4, 1, CH), F32),
            pltpu.VMEM((TAPS, TAPS, CH, CH), BF16),
            pltpu.VMEM((TAPS, TAPS, CH, CH), BF16),
            pltpu.VMEM((TAPS, (ROWS + 4) * COLS, CH), BF16),
            pltpu.VMEM((TAPS, (ROWS + 8) * COLS, CH), BF16),
            pltpu.VMEM((TAPS, (ROWS + 8) * COLS, CH), BF16),
            pltpu.VMEM((TAPS, (ROWS + 4) * COLS, CH), BF16),
            pltpu.VMEM((2, 2 * COLS, CH), BF16),
            pltpu.VMEM((2, 4 * COLS, CH), BF16),
            pltpu.VMEM((2, 4 * COLS, HALF), BF16),
            pltpu.VMEM((2, 4 * COLS, HALF), BF16),
            pltpu.VMEM((2, 2 * COLS, CH), BF16),
            pltpu.VMEM((POS, CH), F32),
            pltpu.VMEM((POS, CH), F32),
            pltpu.VMEM((POS, CH), F32),
            pltpu.VMEM((ROWS, COLS, CH), BF16),
            *[pieces] * 16,
            dma((7,)),
            dma((TAPS,)),
            dma((TAPS,)),
            dma((5, 2)),
            dma((5, 2)),
            dma((4, 2, PEERS)),
            dma((4, 2, PEERS)),
        ],
        compiler_params=pltpu.CompilerParams(
            collective_id=0, has_side_effects=True, vmem_limit_bytes=34 << 20
        ),
        name="distill",
    )(
        *(
            pltpu.with_memory_space_constraint(x, pltpu.HBM)
            for x in (args[2], args[0].reshape(1, POS, CH), args[1], *args[3:])
        )
    )


def solution(mesh):
    placed = (
        P("peer", "space", None, None),
        P("peer", "space", None, None),
        P(),
        P("peer", None, None, None, None),
        P("peer", None),
        P("peer", None),
        P("peer", None, None, None, None),
        P("peer", None),
        P("peer", None),
    )
    return jax.shard_map(
        per_device,
        mesh=mesh,
        in_specs=placed,
        out_specs=P("peer", "space", None, None),
        check_vma=False,
    )
```
